32 devices in a mesh: tm: 16 (over z, y, x), col: 2 (over core).
Axes of the slice: x: 2, y: 2, z: 4, core: 2. Of those that a mesh axis runs over, the one named last changes fastest.
Arguments:
- initial_state: float32 [1024], replicated, may hold values from -6 to 6
- coupling: float32 [1024, 1024], replicated, may hold values from -0.1875 to 0.1875
- modulation: float32 [1024, 1024], replicated, may hold values from -0.1875 to 0.1875
- gains: float32 [16, 5], P('tm'), may hold values from -1 to 1
- forcing: float32 [16, 5, 1024], P('tm'), may hold values from -6 to 6
Outputs:
- slab_ends: float32 [16, 1024], P('tm', 'col')
The draws below stay inside these ranges and needn't reach their ends.
All inputs are finite; a program needn't handle non-finite values.
Results may differ from the reference program's by a relative error of at most 0.0003.
Values sent between devices are 32-bit elements; how exact they have to be, the bound alone decides.
A program may use at most 128 MiB of HBM per device.

```python
import jax
import jax.numpy as jnp
from jax import lax

D = 1024
STEPS = 2
NODES = 5
SLABS = 16


def block_scale(stream_key, dims, split, low, largest):
    def one(dim, parts):
        steps = jax.random.uniform(jax.random.fold_in(jax.random.fold_in(stream_key, 6), dim), (parts,), jnp.float32, low / len(split), largest / len(split))
        return jnp.repeat(jnp.exp(steps), dims[dim] // parts).reshape((-1,) + (1,) * (len(dims) - dim - 1))

    gain = one(*split[0])
    for cut in split[1:]:
        gain = gain * one(*cut)
    return gain


def gaussian(own_key, dims, width, limit, shards=(), kind=jnp.bfloat16):
    entries = jax.random.normal(own_key, dims, jnp.float32) * width
    if len(shards) > 0:
        entries = block_scale(own_key, dims, shards, -0.22, 0.18) * entries
    return jnp.clip(entries, min=-limit, max=limit).astype(kind)


def setup_inputs(seed: int = 0) -> dict:
    key_of = jax.random.split(jax.random.key(seed), 6)
    return {
        "initial_state": gaussian(key_of[0], (D,), 1.0, 6.0, (), jnp.float32),
        "coupling": gaussian(key_of[1], (D, D), D ** -0.5, 0.1875, (), jnp.float32),
        "modulation": gaussian(key_of[2], (D, D), D ** -0.5, 0.1875, (), jnp.float32),
        "gains": jnp.clip(jax.random.uniform(key_of[3], (SLABS, NODES), jnp.float32, -1.0, 1.0) * block_scale(key_of[3], (SLABS, NODES), ((0, 16),), -0.4, 0.0), -1.0, 1.0),
        "forcing": gaussian(key_of[4], (SLABS, NODES, D), 1.0, 6.0, ((0, 16),), jnp.float32),
    }


step_size = 0.1
highest = lax.Precision.HIGHEST


def apply_op(operator, current):
    return jnp.dot(operator, current, precision=highest)


def runge_step(current, op_start, op_mid, op_end, force_start, force_mid, force_end):
    slope_one = apply_op(op_start, current) + force_start
    slope_two = apply_op(op_mid, current + 0.5 * step_size * slope_one) + force_mid
    slope_three = apply_op(op_mid, current + 0.5 * step_size * slope_two) + force_mid
    slope_four = apply_op(op_end, current + step_size * slope_three) + force_end
    return current + (step_size / 6.0) * (slope_one + 2.0 * slope_two + 2.0 * slope_three + slope_four)


def reference(initial_state, coupling, modulation, gains, forcing):
    skew_base = coupling - coupling.T
    skew_vary = modulation - modulation.T

    def advance_slab(current, inputs):
        node_gain, node_force = inputs
        for substep in range(STEPS):
            op_start = skew_base + node_gain[2 * substep] * skew_vary
            op_mid = skew_base + node_gain[2 * substep + 1] * skew_vary
            op_end = skew_base + node_gain[2 * substep + 2] * skew_vary
            current = runge_step(current, op_start, op_mid, op_end, node_force[2 * substep], node_force[2 * substep + 1], node_force[2 * substep + 2])
        return current, current

    finished, slab_ends = lax.scan(advance_slab, initial_state, (gains, forcing))
    return slab_ends
```

```python
import functools

import jax
import jax.numpy as jnp
from jax import lax
from jax.experimental import pallas as pl
from jax.experimental.pallas import tpu as pltpu
from jax.sharding import PartitionSpec as P

step_size = 0.1
highest = lax.Precision.HIGHEST
MESH = pl.DeviceIdType.MESH
f32, bf16 = jnp.float32, jnp.bfloat16


def group_width(devices):
    width = 1
    while width * width < devices:
        width *= 2
    return width


def kernel(
    width, cores, y0_ref, c_hbm, m_hbm, gains_ref, forcing_ref, out_ref,
    cbuf, mbuf, bt, vt, wa_hi, wa_lo, wb_hi, wb_lo, wc_hi, wc_lo,
    x, acc, xs0, xs1, zs, gbuf, fbuf, chain_in, out_in, psend, yv,
    csem, gsend, grecv, vsend, fsend, frecv, chain_send, chain_recv, out_send, out_recv,
):
    rows, size = x.shape
    slabs = zs.shape[0]
    nodes = forcing_ref.shape[1]
    steps = (nodes - 1) // 2
    half = out_ref.shape[1]
    window = chain_in.shape[2]
    tile = min(256, size)
    devices = lax.axis_size("tm") * cores
    groups = devices // width
    me_tm, me_col = lax.axis_index("tm"), lax.axis_index("col")
    flat = me_tm * cores + me_col
    g = flat // width
    p = flat % width
    local = me_tm % slabs
    is_head = g == 0
    is_vec = jnp.logical_and(is_head, p < groups)

    def dev(index):
        return {"tm": index // cores, "col": index % cores}

    def remote(src, dst, send, recv, index):
        return pltpu.make_async_remote_copy(
            src_ref=src, dst_ref=dst, send_sem=send, recv_sem=recv,
            device_id=dev(index), device_id_type=MESH,
        )

    load_c = pltpu.make_async_copy(c_hbm, cbuf, csem.at[0])
    load_m = pltpu.make_async_copy(m_hbm, mbuf, csem.at[1])
    load_c.start()
    load_m.start()

    gbuf[...] = jnp.zeros_like(gbuf)
    fbuf[...] = jnp.zeros_like(fbuf)

    barrier = pltpu.get_barrier_semaphore()

    @pl.loop(1, devices)
    def _(o):
        pl.semaphore_signal(barrier, inc=1, device_id=dev((flat + o) % devices), device_id_type=MESH)

    pl.semaphore_wait(barrier, devices - 1)

    def mate_gain(o):
        target = (g * slabs + (local + o) % slabs) * cores + me_col
        return remote(gains_ref, gbuf.at[local], gsend.at[o], grecv.at[local], target)

    def vec_gain():
        return remote(gains_ref, gbuf.at[local], vsend.at[0], grecv.at[local], g)

    def vec_force():
        return remote(forcing_ref.at[0], fbuf.at[local], fsend.at[0], frecv.at[local], g)

    feeds_vec = jnp.logical_and(me_col == 0, flat != 0)

    @pl.when(jnp.logical_not(is_head))
    def _():
        gbuf[local] = gains_ref[...]
        for o in range(1, slabs):
            mate_gain(o).start()

    @pl.when(feeds_vec)
    def _():
        vec_gain().start()
        vec_force().start()

    @pl.when(flat == 0)
    def _():
        gbuf[0] = gains_ref[...]
        fbuf[0] = forcing_ref[0]

    row_id = lax.broadcasted_iota(jnp.int32, (rows, tile), 0)
    col_id = lax.broadcasted_iota(jnp.int32, (rows, tile), 1)

    for n in range(size // tile):
        ns = slice(n * tile, (n + 1) * tile)
        eye = jnp.where(col_id + n * tile == row_id + p * rows, 1.0, 0.0).astype(f32)
        first = jnp.where(jnp.logical_and(row_id == 0, p == 0), y0_ref[:, ns], 0.0)
        start = jnp.where(is_head, first, eye)
        x[:, ns] = start
        hi = start.astype(bf16)
        xs0[:rows, ns] = hi
        xs0[rows:, ns] = (start - hi.astype(f32)).astype(bf16)

    def skew(src, dst):
        @pl.loop(0, size // 128)
        def _(i):
            blk = pl.ds(pl.multiple_of(i * 128, 128), 128)
            dst[blk, :] = src[:, blk].T - src[blk, :]

    load_c.wait()
    skew(cbuf, bt)
    load_m.wait()
    skew(mbuf, vt)

    for i in range(slabs):
        @pl.when(jnp.logical_or(
            jnp.logical_and(jnp.logical_not(is_head), local != i),
            jnp.logical_and(is_vec, flat + i != 0),
        ))
        def _(i=i):
            remote(gains_ref, gbuf.at[i], gsend.at[0], grecv.at[i], 0).wait_recv()

        @pl.when(jnp.logical_and(is_vec, flat + i != 0))
        def _(i=i):
            remote(forcing_ref.at[0], fbuf.at[i], fsend.at[0], frecv.at[i], 0).wait_recv()

    pieces = max(1, size // 128)

    def form(ns, gain, w_hi, w_lo):
        for k in range(pieces):
            ks = slice(k * size // pieces, (k + 1) * size // pieces)
            w = bt[ks, ns] + gain * vt[ks, ns]
            hi = w.astype(bf16)
            w_hi[ks, ns] = hi
            w_lo[ks, ns] = (w - hi.astype(f32)).astype(bf16)

    wa, wb, wc = (wa_hi, wa_lo), (wb_hi, wb_lo), (wc_hi, wc_lo)

    def gain_of(slab, node):
        return gbuf[slab][:, node:node + 1]

    @pl.loop(0, size // tile)
    def _(n):
        form(pl.ds(pl.multiple_of(n * tile, tile), tile), gain_of(0, 0), *wc)

    h = step_size
    push = jnp.logical_and(row_id == 0, is_head)

    def stage(slab, kind, node, w, source, target, following):
        @pl.loop(0, size // tile)
        def _(n):
            ns = pl.ds(pl.multiple_of(n * tile, tile), tile)
            both = jnp.dot(source[...], w[0][:, ns], preferred_element_type=f32)
            k = both[:rows] + both[rows:]
            k = k + jnp.dot(source[:rows, :], w[1][:, ns], preferred_element_type=f32)
            k = k + jnp.where(push, fbuf[slab, node:node + 1, ns], 0.0)
            now = x[:, ns]
            if kind == 0:
                acc[:, ns] = now + (h / 6.0) * k
                arg = now + (0.5 * h) * k
            elif kind == 1:
                acc[:, ns] += (h / 3.0) * k
                arg = now + (0.5 * h) * k
            elif kind == 2:
                acc[:, ns] += (h / 3.0) * k
                arg = now + h * k
            else:
                arg = acc[:, ns] + (h / 6.0) * k
                x[:, ns] = arg
                if node == nodes - 1:
                    zs[slab, :, ns] = arg
            hi = arg.astype(bf16)
            target[:rows, ns] = hi
            target[rows:, ns] = (arg - hi.astype(f32)).astype(bf16)
            if following is not None:
                form(ns, following[0], *following[1])

    @pl.loop(0, slabs)
    def _(slab):
        after = jnp.minimum(slab + 1, slabs - 1)
        for step in range(steps):
            w0 = wc if step == 0 else wa
            base = 2 * step
            last = step == steps - 1
            stage(slab, 0, base, w0, xs0, xs1, (gain_of(slab, base + 1), wb) if step == 0 else None)
            stage(slab, 1, base + 1, wb, xs1, xs0, (gain_of(slab, base + 2), wa))
            stage(slab, 2, base + 1, wb, xs0, xs1, None)
            stage(slab, 3, base + 2, wa, xs1, xs0, (gain_of(after, 0), wc) if last else (gain_of(slab, base + 3), wb))

    def start_of(q):
        return q * rows // 128 * 128

    def to_chain(q):
        slot = jnp.where(is_head, width, p)
        index = jnp.where(is_head, p + 1, g + 1) * width + q
        src = psend.at[slabs - 1, :, pl.ds(start_of(q), window)]
        return remote(src, chain_in.at[slot], chain_send.at[q], chain_recv.at[slot], index)

    def to_out(o):
        d = (p + o) % width
        src = psend.at[d // cores, :, pl.ds(pl.multiple_of(d % cores * half, half), half)]
        return remote(src, out_in.at[p], out_send.at[o], out_recv.at[p], g * width + d)

    def head_out(d):
        src = psend.at[d // cores, :, pl.ds(d % cores * half, half)]
        return remote(src, out_in.at[width], out_send.at[d], out_recv.at[width], p * width + d)

    def chain_wait(slot):
        remote(psend.at[0, :, pl.ds(0, window)], chain_in.at[slot], chain_send.at[0], chain_recv.at[slot], 0).wait_recv()

    def out_wait(slot):
        remote(psend.at[0, :, pl.ds(0, half)], out_in.at[slot], out_send.at[0], out_recv.at[slot], 0).wait_recv()

    @pl.when(is_vec)
    def _():
        for s in range(slabs):
            psend[s] = zs[s, 0:1, :]

        @pl.when(p + 1 < groups)
        def _():
            for q in range(width):
                to_chain(q).start()

        for d in range(width):
            if d == 0:
                @pl.when(p == 0)
                def _():
                    out_in[width] = psend[0][:, :half]

                @pl.when(p != 0)
                def _():
                    head_out(0).start()
            else:
                head_out(d).start()

    @pl.when(is_head)
    def _():
        @pl.when(p != 0)
        def _():
            out_wait(width)

        out_ref[...] = out_in[width]

    @pl.when(jnp.logical_not(is_head))
    def _():
        chain_wait(width)
        yv[...] = chain_in[width]

        @pl.when(g > 1)
        def _():
            for q in range(width):
                chain_wait(q)
            total = yv[...]
            for q in range(width):
                total = total + chain_in[q]
            yv[...] = total

        begin = yv[...]
        if rows < window:
            part = begin[:, :rows]
            for i in range(1, window // rows):
                part = jnp.where(p % (window // rows) == i, begin[:, i * rows:(i + 1) * rows], part)
            begin = part
        begin = jnp.broadcast_to(begin, (8, rows))

        def apply_map(s):
            psend[s] = jnp.dot(begin, zs[s], precision=highest, preferred_element_type=f32)[0:1, :]

        apply_map(slabs - 1)

        @pl.when(g + 1 < groups)
        def _():
            for q in range(width):
                to_chain(q).start()

        for s in range(slabs - 1):
            apply_map(s)
        for o in range(1, width):
            to_out(o).start()
        own = psend[p // cores]
        mine = own[:, :half]
        for c in range(1, cores):
            mine = jnp.where(me_col == c, own[:, c * half:(c + 1) * half], mine)
        out_wait(width)
        mine = mine + out_in[width]
        for o in range(1, width):
            q = (p + o) % width
            out_wait(q)
            mine = mine + out_in[q]
        out_ref[...] = mine
        for o in range(1, width):
            to_out(o).wait_send()
        for o in range(1, slabs):
            mate_gain(o).wait_send()

        @pl.when(g + 1 < groups)
        def _():
            for q in range(width):
                to_chain(q).wait_send()

    @pl.when(is_vec)
    def _():
        @pl.when(p + 1 < groups)
        def _():
            for q in range(width):
                to_chain(q).wait_send()

        @pl.when(p != 0)
        def _():
            head_out(0).wait_send()

        for d in range(1, width):
            head_out(d).wait_send()

    @pl.when(feeds_vec)
    def _():
        vec_gain().wait_send()
        vec_force().wait_send()


def shards(initial_state, coupling, modulation, gains, forcing):
    size = coupling.shape[0]
    cores = lax.axis_size("col")
    devices = lax.axis_size("tm") * cores
    width = group_width(devices)
    rows = size // width
    slabs = width // cores
    nodes = gains.shape[1]
    half = size // cores
    window = max(128, rows)
    vmem = pltpu.VMEM
    dma = pltpu.SemaphoreType.DMA
    mat32, mat16 = vmem((size, size), f32), vmem((size, size), bf16)
    return pl.pallas_call(
        functools.partial(kernel, width, cores),
        out_shape=jax.ShapeDtypeStruct((1, half), f32),
        in_specs=[
            pl.BlockSpec(memory_space=vmem),
            pl.BlockSpec(memory_space=pl.ANY),
            pl.BlockSpec(memory_space=pl.ANY),
            pl.BlockSpec(memory_space=vmem),
            pl.BlockSpec(memory_space=vmem),
        ],
        out_specs=pl.BlockSpec(memory_space=vmem),
        scratch_shapes=[
            mat32, mat32, mat32, mat32,
            mat16, mat16, mat16, mat16, mat16, mat16,
            vmem((rows, size), f32),
            vmem((rows, size), f32),
            vmem((2 * rows, size), bf16),
            vmem((2 * rows, size), bf16),
            vmem((slabs, rows, size), f32),
            vmem((slabs, 1, nodes), f32),
            vmem((slabs, nodes, size), f32),
            vmem((width + 1, 1, window), f32),
            vmem((width + 1, 1, half), f32),
            vmem((slabs, 1, size), f32),
            vmem((1, window), f32),
            dma((2,)), dma((slabs,)), dma((slabs,)), dma((1,)), dma((1,)), dma((slabs,)),
            dma((width,)), dma((width + 1,)), dma((width,)), dma((width + 1,)),
        ],
        compiler_params=pltpu.CompilerParams(
            collective_id=0, has_side_effects=True, vmem_limit_bytes=60 * 1024 * 1024
        ),
    )(initial_state[None, :], coupling, modulation, gains, forcing)


def solution(mesh):
    in_specs = (P(), P(), P(), P("tm", None), P("tm", None, None))
    out_specs = P("tm", "col")
    return jax.shard_map(shards, mesh=mesh, in_specs=in_specs, out_specs=out_specs, check_vma=False)
```

```python
import functools

import jax
import jax.numpy as jnp
from jax import lax
from jax.experimental import pallas as pl
from jax.experimental.pallas import tpu as pltpu
from jax.sharding import PartitionSpec as P

step_size = 0.1
highest = lax.Precision.HIGHEST
MESH = pl.DeviceIdType.MESH
f32, bf16 = jnp.float32, jnp.bfloat16


def group_width(devices):
    width = 1
    while width * width < devices:
        width *= 2
    return width


def kernel(
    width, cores, y0_ref, c_hbm, m_hbm, gains_ref, forcing_ref, out_ref,
    cbuf, mbuf, bt, vt, w_hi, w_lo,
    x, acc, xs0, xs1, zs, gbuf, fbuf, chain_in, out_in, psend, yv,
    csem, gsend, grecv, vsend, fsend, frecv, chain_send, chain_recv, out_send, out_recv,
):
    rows, size = x.shape
    slabs = zs.shape[0]
    nodes = forcing_ref.shape[1]
    steps = (nodes - 1) // 2
    half = out_ref.shape[1]
    window = chain_in.shape[2]
    tile = min(1024, size)
    devices = lax.axis_size("tm") * cores
    groups = devices // width
    me_tm, me_col = lax.axis_index("tm"), lax.axis_index("col")
    flat = me_tm * cores + me_col
    g = flat // width
    p = flat % width
    local = me_tm % slabs
    is_head = g == 0
    is_vec = jnp.logical_and(is_head, p < groups)

    def dev(index):
        return {"tm": index // cores, "col": index % cores}

    def remote(src, dst, send, recv, index):
        return pltpu.make_async_remote_copy(
            src_ref=src, dst_ref=dst, send_sem=send, recv_sem=recv,
            device_id=dev(index), device_id_type=MESH,
        )

    load_c = pltpu.make_async_copy(c_hbm, cbuf, csem.at[0])
    load_m = pltpu.make_async_copy(m_hbm, mbuf, csem.at[1])
    load_c.start()
    load_m.start()

    gbuf[...] = jnp.zeros_like(gbuf)
    fbuf[...] = jnp.zeros_like(fbuf)

    barrier = pltpu.get_barrier_semaphore()

    @pl.loop(1, devices)
    def _(o):
        pl.semaphore_signal(barrier, inc=1, device_id=dev((flat + o) % devices), device_id_type=MESH)

    pl.semaphore_wait(barrier, devices - 1)

    def mate_gain(o):
        target = (g * slabs + (local + o) % slabs) * cores + me_col
        return remote(gains_ref, gbuf.at[local], gsend.at[o], grecv.at[local], target)

    def vec_gain():
        return remote(gains_ref, gbuf.at[local], vsend.at[0], grecv.at[local], g)

    def vec_force():
        return remote(forcing_ref.at[0], fbuf.at[local], fsend.at[0], frecv.at[local], g)

    feeds_vec = jnp.logical_and(me_col == 0, flat != 0)

    @pl.when(jnp.logical_not(is_head))
    def _():
        gbuf[local] = gains_ref[...]
        for o in range(1, slabs):
            mate_gain(o).start()

    @pl.when(feeds_vec)
    def _():
        vec_gain().start()
        vec_force().start()

    @pl.when(flat == 0)
    def _():
        gbuf[0] = gains_ref[...]
        own_force = pltpu.make_async_copy(forcing_ref.at[0], fbuf.at[0], csem.at[2])
        own_force.start()
        own_force.wait()

    row_id = lax.broadcasted_iota(jnp.int32, (rows, tile), 0)
    col_id = lax.broadcasted_iota(jnp.int32, (rows, tile), 1)

    for n in range(size // tile):
        ns = slice(n * tile, (n + 1) * tile)
        eye = jnp.where(col_id + n * tile == row_id + p * rows, 1.0, 0.0).astype(f32)
        first = jnp.where(jnp.logical_and(row_id == 0, p == 0), y0_ref[:, ns], 0.0)
        start = jnp.where(is_head, first, eye)
        x[:, ns] = start
        hi = start.astype(bf16)
        xs0[:rows, ns] = hi
        xs0[rows:, ns] = (start - hi.astype(f32)).astype(bf16)

    def skew(src, dst):
        @pl.loop(0, size // 128)
        def _(i):
            blk = pl.ds(pl.multiple_of(i * 128, 128), 128)
            dst[blk, :] = src[:, blk].T - src[blk, :]

    load_c.wait()
    skew(cbuf, bt)
    load_m.wait()
    skew(mbuf, vt)

    for i in range(slabs):
        @pl.when(jnp.logical_or(
            jnp.logical_and(jnp.logical_not(is_head), local != i),
            jnp.logical_and(is_vec, flat + i != 0),
        ))
        def _(i=i):
            remote(gains_ref, gbuf.at[i], gsend.at[0], grecv.at[i], 0).wait_recv()

        @pl.when(jnp.logical_and(is_vec, flat + i != 0))
        def _(i=i):
            remote(forcing_ref.at[0], fbuf.at[i], fsend.at[0], frecv.at[i], 0).wait_recv()

    pieces = max(1, size // 128)

    def form(ns, gain, keep):
        his, los = [], []
        for k in range(pieces):
            ks = slice(k * size // pieces, (k + 1) * size // pieces)
            w = bt[ks, ns] + gain * vt[ks, ns]
            hi = w.astype(bf16)
            lo = (w - hi.astype(f32)).astype(bf16)
            his.append(hi)
            los.append(lo)
            if keep:
                w_hi[ks, ns] = hi
                w_lo[ks, ns] = lo
        return jnp.concatenate(his, axis=0), jnp.concatenate(los, axis=0)

    def gain_of(slab, node):
        return gbuf[slab][:, node:node + 1]

    h = step_size
    push = jnp.logical_and(row_id == 0, is_head)

    def stage(slab, kind, node, fresh, keep, source, target):
        @pl.loop(0, size // tile)
        def _(n):
            ns = pl.ds(pl.multiple_of(n * tile, tile), tile)
            if fresh:
                hi, lo = form(ns, gain_of(slab, node), keep)
            else:
                hi, lo = w_hi[:, ns], w_lo[:, ns]
            both = jnp.dot(source[...], hi, preferred_element_type=f32)
            k = both[:rows] + both[rows:]
            k = k + jnp.dot(source[:rows, :], lo, preferred_element_type=f32)
            k = k + jnp.where(push, fbuf[slab, node:node + 1, ns], 0.0)
            now = x[:, ns]
            if kind == 0:
                acc[:, ns] = now + (h / 6.0) * k
                arg = now + (0.5 * h) * k
            elif kind == 1:
                acc[:, ns] += (h / 3.0) * k
                arg = now + (0.5 * h) * k
            elif kind == 2:
                acc[:, ns] += (h / 3.0) * k
                arg = now + h * k
            else:
                arg = acc[:, ns] + (h / 6.0) * k
                x[:, ns] = arg
                if node == nodes - 1:
                    zs[slab, :, ns] = arg
            hi = arg.astype(bf16)
            target[:rows, ns] = hi
            target[rows:, ns] = (arg - hi.astype(f32)).astype(bf16)

    @pl.loop(0, slabs)
    def _(slab):
        for step in range(steps):
            base = 2 * step
            stage(slab, 0, base, step == 0, False, xs0, xs1)
            stage(slab, 1, base + 1, True, True, xs1, xs0)
            stage(slab, 2, base + 1, False, False, xs0, xs1)
            stage(slab, 3, base + 2, True, step < steps - 1, xs1, xs0)

    def start_of(q):
        return q * rows // 128 * 128

    def to_chain(q):
        slot = jnp.where(is_head, width, p)
        index = jnp.where(is_head, p + 1, g + 1) * width + q
        src = psend.at[slabs - 1, :, pl.ds(start_of(q), window)]
        return remote(src, chain_in.at[slot], chain_send.at[q], chain_recv.at[slot], index)

    def to_out(o):
        d = (p + o) % width
        src = psend.at[d // cores, :, pl.ds(pl.multiple_of(d % cores * half, half), half)]
        return remote(src, out_in.at[p], out_send.at[o], out_recv.at[p], g * width + d)

    def head_out(d):
        src = psend.at[d // cores, :, pl.ds(d % cores * half, half)]
        return remote(src, out_in.at[width], out_send.at[d], out_recv.at[width], p * width + d)

    def chain_wait(slot):
        remote(psend.at[0, :, pl.ds(0, window)], chain_in.at[slot], chain_send.at[0], chain_recv.at[slot], 0).wait_recv()

    def out_wait(slot):
        remote(psend.at[0, :, pl.ds(0, half)], out_in.at[slot], out_send.at[0], out_recv.at[slot], 0).wait_recv()

    @pl.when(is_vec)
    def _():
        for s in range(slabs):
            psend[s] = zs[s, 0:1, :]

        @pl.when(p + 1 < groups)
        def _():
            for q in range(width):
                to_chain(q).start()

        for d in range(width):
            if d == 0:
                @pl.when(p == 0)
                def _():
                    out_in[width] = psend[0][:, :half]

                @pl.when(p != 0)
                def _():
                    head_out(0).start()
            else:
                head_out(d).start()

    @pl.when(is_head)
    def _():
        @pl.when(p != 0)
        def _():
            out_wait(width)

        out_ref[...] = out_in[width]

    @pl.when(jnp.logical_not(is_head))
    def _():
        chain_wait(width)
        yv[...] = chain_in[width]

        @pl.when(g > 1)
        def _():
            for q in range(width):
                chain_wait(q)
            total = yv[...]
            for q in range(width):
                total = total + chain_in[q]
            yv[...] = total

        begin = yv[...]
        if rows < window:
            part = begin[:, :rows]
            for i in range(1, window // rows):
                part = jnp.where(p % (window // rows) == i, begin[:, i * rows:(i + 1) * rows], part)
            begin = part
        begin = jnp.broadcast_to(begin, (8, rows))

        def apply_map(s):
            psend[s] = jnp.dot(begin, zs[s], precision=highest, preferred_element_type=f32)[0:1, :]

        apply_map(slabs - 1)

        @pl.when(g + 1 < groups)
        def _():
            for q in range(width):
                to_chain(q).start()

        for s in range(slabs - 1):
            apply_map(s)
        for o in range(1, width):
            to_out(o).start()
        own = psend[p // cores]
        mine = own[:, :half]
        for c in range(1, cores):
            mine = jnp.where(me_col == c, own[:, c * half:(c + 1) * half], mine)
        out_wait(width)
        mine = mine + out_in[width]
        for o in range(1, width):
            q = (p + o) % width
            out_wait(q)
            mine = mine + out_in[q]
        out_ref[...] = mine
        for o in range(1, width):
            to_out(o).wait_send()
        for o in range(1, slabs):
            mate_gain(o).wait_send()

        @pl.when(g + 1 < groups)
        def _():
            for q in range(width):
                to_chain(q).wait_send()

    @pl.when(is_vec)
    def _():
        @pl.when(p + 1 < groups)
        def _():
            for q in range(width):
                to_chain(q).wait_send()

        @pl.when(p != 0)
        def _():
            head_out(0).wait_send()

        for d in range(1, width):
            head_out(d).wait_send()

    @pl.when(feeds_vec)
    def _():
        vec_gain().wait_send()
        vec_force().wait_send()


def shards(initial_state, coupling, modulation, gains, forcing):
    size = coupling.shape[0]
    cores = lax.axis_size("col")
    devices = lax.axis_size("tm") * cores
    width = group_width(devices)
    rows = size // width
    slabs = width // cores
    nodes = gains.shape[1]
    half = size // cores
    window = max(128, rows)
    vmem = pltpu.VMEM
    dma = pltpu.SemaphoreType.DMA
    mat32, mat16 = vmem((size, size), f32), vmem((size, size), bf16)
    return pl.pallas_call(
        functools.partial(kernel, width, cores),
        out_shape=jax.ShapeDtypeStruct((1, half), f32),
        in_specs=[
            pl.BlockSpec(memory_space=vmem),
            pl.BlockSpec(memory_space=pl.ANY),
            pl.BlockSpec(memory_space=pl.ANY),
            pl.BlockSpec(memory_space=vmem),
            pl.BlockSpec(memory_space=pl.ANY),
        ],
        out_specs=pl.BlockSpec(memory_space=vmem),
        scratch_shapes=[
            mat32, mat32, mat32, mat32,
            mat16, mat16,
            vmem((rows, size), f32),
            vmem((rows, size), f32),
            vmem((2 * rows, size), bf16),
            vmem((2 * rows, size), bf16),
            vmem((slabs, rows, size), f32),
            vmem((slabs, 1, nodes), f32),
            vmem((slabs, nodes, size), f32),
            vmem((width + 1, 1, window), f32),
            vmem((width + 1, 1, half), f32),
            vmem((slabs, 1, size), f32),
            vmem((1, window), f32),
            dma((3,)), dma((slabs,)), dma((slabs,)), dma((1,)), dma((1,)), dma((slabs,)),
            dma((width,)), dma((width + 1,)), dma((width,)), dma((width + 1,)),
        ],
        compiler_params=pltpu.CompilerParams(
            collective_id=0, has_side_effects=True, vmem_limit_bytes=60 * 1024 * 1024
        ),
    )(initial_state[None, :], coupling, modulation, gains, forcing)


def solution(mesh):
    in_specs = (P(), P(), P(), P("tm", None), P("tm", None, None))
    out_specs = P("tm", "col")
    return jax.shard_map(shards, mesh=mesh, in_specs=in_specs, out_specs=out_specs, check_vma=False)
```
